1024 devices in a mesh: stn: 256 (over y_lo, z, x, core), elem: 4 (over y_hi).
Axes of the slice: x: 8, y: 8 (y_hi: 4, y_lo: 2; y = y_hi * 2 + y_lo), z: 8, core: 2. Of those that a mesh axis runs over, the one named last changes fastest.
Arguments:
- voltages: bfloat16 [2, 256, 64, 16, 128], P(None, 'stn', 'elem'), may hold values from -6 to 6
- weights: bfloat16 [2, 8, 64, 16], P(None, None, 'elem'), may hold values from -0.5 to 0.5
Outputs:
- spectra: float32 [2, 16, 2048, 2048], P(None, 'elem', 'stn')
The draws below stay inside these ranges and needn't reach their ends.
All inputs are finite; a program needn't handle non-finite values.
Results may differ from the reference program's by a relative error of at most 0.0075.
Values may be sent and summed in bfloat16 or wider, within the bound.
A program may use at most 32 MiB of HBM per device.

```python
import jax
import jax.numpy as jnp
from jax import lax

ELEMS = 64
NB = 8
CH = 16
T_SIZE = 128
STATIONS = 256
BEAMS = 2048


def level_of(rng, shape, cuts, least, high):
    def one(position, parts):
        heights = jax.random.uniform(jax.random.fold_in(jax.random.fold_in(rng, 6), position), (parts,), jnp.float32, least / len(cuts), high / len(cuts))
        return jnp.repeat(jnp.exp(heights), shape[position] // parts).reshape((-1,) + (1,) * (len(shape) - position - 1))

    gain = one(*cuts[0])
    for cut in cuts[1:]:
        gain = gain * one(*cut)
    return gain


def centred(stream_key, dims, scale, bound, shards=(), held_as=jnp.bfloat16):
    drawn = scale * jax.random.normal(stream_key, dims, jnp.float32)
    if shards:
        drawn = drawn * level_of(stream_key, dims, shards, -0.22, 0.18)
    return jnp.clip(drawn, -bound, bound).astype(held_as)


def setup_inputs(seed: int = 0) -> dict:
    streams_of = jax.random.split(jax.random.key(seed), 3)
    voltages = centred(streams_of[0], (2, STATIONS, ELEMS, CH, T_SIZE), 1.0, 6.0, ((1, 256), (2, 4)))
    weights = centred(streams_of[1], (2, NB, ELEMS, CH), (2 * ELEMS) ** -0.5, 0.5, ((2, 4),))
    return dict(voltages=voltages, weights=weights)


def reference(voltages, weights):
    volt_real = voltages[0].astype(jnp.float32)
    volt_imag = voltages[1].astype(jnp.float32)
    weight_real = weights[0].astype(jnp.float32)
    weight_imag = weights[1].astype(jnp.float32)
    beam_real = jnp.einsum("kec,sect->sckt", weight_real, volt_real) + jnp.einsum("kec,sect->sckt", weight_imag, volt_imag)
    beam_imag = jnp.einsum("kec,sect->sckt", weight_real, volt_imag) - jnp.einsum("kec,sect->sckt", weight_imag, volt_real)
    stacked = jnp.stack([beam_real, beam_imag]).astype(jnp.bfloat16)
    stacked = jnp.transpose(stacked, (0, 2, 1, 3, 4)).reshape(2, CH, BEAMS, T_SIZE)

    def one_channel(pair):
        left_real, left_imag = pair
        spec_real = jnp.dot(left_real, left_real.T, preferred_element_type=jnp.float32) + jnp.dot(left_imag, left_imag.T, preferred_element_type=jnp.float32)
        spec_imag = jnp.dot(left_imag, left_real.T, preferred_element_type=jnp.float32) - jnp.dot(left_real, left_imag.T, preferred_element_type=jnp.float32)
        return jnp.stack([spec_real, spec_imag]) / jnp.float32(T_SIZE)

    result = lax.map(one_channel, (stacked[0], stacked[1]))
    return jnp.transpose(result, (1, 0, 2, 3))
```

```python
import functools

import jax
import jax.numpy as jnp
from jax import lax
from jax.experimental import pallas as pl
from jax.experimental.pallas import tpu as pltpu
from jax.sharding import PartitionSpec as P

MESH = pl.DeviceIdType.MESH
F32, BF16 = jnp.float32, jnp.bfloat16
RING, YS, CORES, PARTS = 8, 2, 2, 4
NB, CH, HALF = 8, 16, 2
PLANE = YS * RING
FAR = (4, 3, 5, 2, 6, 1, 7)


def iota(shape, dim):
    return lax.broadcasted_iota(jnp.int32, shape, dim)


def beam_matrix(w_ref):
    elems = w_ref.shape[1] // NB
    spread = (iota((CH, elems * CH), 1) % CH == iota((CH, elems * CH), 0)).astype(F32).astype(BF16)
    shape = (NB * elems, elems * CH)
    own = iota(shape, 0) % elems == iota(shape, 1) // CH
    shape = (2 * NB, NB * elems)
    pick = (iota(shape, 0) % NB == iota(shape, 1) // elems).astype(F32).astype(BF16)
    flat = []
    for part in range(2):
        wide = jnp.dot(w_ref[part], spread, preferred_element_type=F32)
        wide = jnp.where(own, wide, 0.0).astype(BF16)
        flat.append(jnp.dot(pick, wide, preferred_element_type=F32))
    top = iota(flat[0].shape, 0) < NB
    left = jnp.where(top, flat[0], -flat[1])
    right = jnp.where(top, flat[1], flat[0])
    both = jnp.concatenate([left, right], axis=1)
    lane = iota(both.shape, 1) % CH
    return jnp.concatenate(
        [jnp.where(lane == c, both, 0.0).astype(BF16) for c in range(CH)], axis=0
    )


def kernel(scale, volt_hbm, w_hbm, out_ref, volt, w, part32, part16, got, mine, cols, rows, res, ret,
           in_sem, es_sem, er_sem, gs_sem, cr_sem, rr_sem, ts_sem, tr_sem):
    s, e = lax.axis_index("stn"), lax.axis_index("elem")
    k, x = lax.rem(s, 2), lax.rem(s // 2, RING)
    z, y = lax.rem(s // (2 * RING), RING), s // (2 * RING * RING)

    def at(yy, zz, xx, kk):
        return {"stn": ((yy * RING + zz) * RING + xx) * 2 + kk, "elem": e}

    def on_ring(h, d, kk):
        return at(y, z, lax.rem(x + d, RING), kk) if h == 0 else at(y, lax.rem(z + d, RING), x, kk)

    def on_plane(h, dy, d, kk):
        yy = lax.rem(y + dy, YS)
        if h == 0:
            return at(yy, lax.rem(z + d, RING), x, kk)
        return at(yy, z, lax.rem(x + d, RING), kk)

    r_own, w_own = x + k * (z - x), z + k * (x - z)

    def my_plane(dy, d, kk):
        yy = lax.rem(y + dy, YS)
        ww = lax.rem(w_own + d, RING)
        return at(yy, ww + k * (z - ww), x + k * (ww - x), kk)

    def my_ring(d, kk):
        rr = lax.rem(r_own + d, RING)
        return at(y, z + k * (rr - z), rr + k * (x - rr), kk)

    partner = at(y, z, x, 1 - k)
    plane_steps = [(dy, d) for dy in (1, 0) for d in FAR + (0,) if (dy, d) != (0, 0)]

    barrier = pltpu.get_barrier_semaphore()
    peers = 0

    def greet(device):
        nonlocal peers
        pl.semaphore_signal(barrier, inc=1, device_id=device, device_id_type=MESH)
        peers += 1

    for d in range(1, PARTS):
        greet({"stn": s, "elem": lax.rem(e + d, PARTS)})
    greet(partner)
    for dy, d in plane_steps:
        greet(my_plane(dy, d, k))
        greet(my_plane(dy, d, 1 - k))
    for dy, d in plane_steps:
        yy = lax.rem(y + dy, YS)
        rr = lax.rem(r_own + d, RING)
        greet(at(yy, z + k * (rr - z), rr + k * (x - rr), 1 - k))
    for d in FAR:
        greet(my_ring(d, k))

    load_v = pltpu.make_async_copy(volt_hbm, volt, in_sem.at[0])
    load_w = pltpu.make_async_copy(w_hbm, w, in_sem.at[1])
    load_w.start()
    load_v.start()
    load_w.wait()
    matrix = beam_matrix(w)
    load_v.wait()
    partial = jnp.dot(matrix, volt[...], preferred_element_type=F32)
    part32[...] = partial
    part16[...] = partial.astype(part16.dtype)
    pl.semaphore_wait(barrier, peers)

    quarter = part32.shape[0] // PARTS
    sends = []
    for d in (2, 1, 3):
        q = lax.rem(e + d, PARTS)
        copy = pltpu.make_async_remote_copy(
            src_ref=part16.at[pl.ds(pl.multiple_of(q * quarter, quarter), quarter)],
            dst_ref=got.at[d - 1],
            send_sem=es_sem.at[d - 1],
            recv_sem=er_sem.at[d - 1],
            device_id={"stn": s, "elem": q},
            device_id_type=MESH,
        )
        copy.start()
        sends.append(copy)
    total = part32[pl.ds(pl.multiple_of(e * quarter, quarter), quarter)]
    for copy, d in zip(sends, (2, 1, 3)):
        copy.wait_recv()
    for d in (1, 2, 3):
        total = total + got[d - 1].astype(F32)
    beams = total.astype(BF16).reshape(mine.shape)
    mine[...] = beams

    count = 0

    def send(src, dst, sem, device):
        nonlocal count
        copy = pltpu.make_async_remote_copy(
            src_ref=src, dst_ref=dst, send_sem=gs_sem.at[count], recv_sem=sem,
            device_id=device, device_id_type=MESH,
        )
        copy.start()
        sends.append(copy)
        count += 1

    coord = ((x, z), (z, x))
    for d in FAR:
        for h in range(2):
            slot = coord[h][0] * 2 + k
            send(mine.at[h], cols.at[slot], cr_sem.at[slot], on_ring(h, d, h))
    for dy, d in plane_steps:
        for h in range(2):
            slot = (y * RING + coord[h][1]) * 2 + k
            send(mine.at[h], rows.at[slot], rr_sem.at[slot], on_plane(h, dy, d, h))
    slot = w_own * 2 + k
    send(mine.at[1 - k], cols.at[slot], cr_sem.at[slot], partner)
    slot = (y * RING + r_own) * 2 + k
    send(mine.at[1 - k], rows.at[slot], rr_sem.at[slot], partner)
    own = mine[k]
    own_col, own_row = r_own * 2, (y * RING + w_own) * 2
    cols[own_col + k] = own
    rows[own_row + k] = own

    def landed(dst, sem):
        pltpu.make_async_remote_copy(
            src_ref=dst, dst_ref=dst, send_sem=gs_sem.at[0], recv_sem=sem,
            device_id=partner, device_id_type=MESH,
        ).wait_recv()

    landed(cols.at[own_col + 1 - k], cr_sem.at[own_col + 1 - k])
    for d in range(1, RING):
        for kk in range(2):
            slot = lax.rem(r_own + d, RING) * 2 + kk
            landed(cols.at[slot], cr_sem.at[slot])
    col_parts = []
    for c in range(HALF):
        wide = cols[:, c].astype(F32).reshape(RING * CORES, 2, NB, -1)
        col_parts.append(tuple(
            wide[:, part].reshape(RING * CORES * NB, -1).astype(BF16) for part in range(2)
        ))

    back = 0
    for dy in range(YS):
        yy = lax.rem(y + dy, YS)
        base = yy * RING * CORES
        for d in range(RING):
            slot = base + lax.rem(w_own + d, RING) * 2
            if (dy, d) == (0, 0):
                landed(rows.at[slot + 1 - k], rr_sem.at[slot + 1 - k])
            else:
                for kk in range(2):
                    landed(rows.at[slot + kk], rr_sem.at[slot + kk])
        block = pl.ds(base, RING * CORES)
        for c in range(HALF):
            tile = rows[block, c]
            n, _, samples = tile.shape
            wide = tile.astype(F32).reshape(n, 2, NB, samples)
            turned = jnp.concatenate([wide[:, 1:], -wide[:, :1]], axis=1)
            turned = turned.reshape(n * 2 * NB, samples).astype(BF16)
            tile = tile.reshape(n * 2 * NB, samples)
            cross = (((1,), (1,)), ((), ()))
            prod = lax.dot_general(tile, col_parts[c][0], cross, preferred_element_type=F32)
            prod += lax.dot_general(turned, col_parts[c][1], cross, preferred_element_type=F32)
            res[block, c] = (prod * scale).astype(BF16).reshape(n, 2 * NB, -1)
        here = y * RING + w_own
        for d in FAR + (0,):
            slot = base + lax.rem(w_own + d, RING) * 2
            if (dy, d) == (0, 0):
                kinds = (1 - k,)
            else:
                kinds = (0, 1)
            for kk in kinds:
                copy = pltpu.make_async_remote_copy(
                    src_ref=res.at[slot + kk], dst_ref=ret.at[k, here], send_sem=ts_sem.at[back],
                    recv_sem=tr_sem.at[k, here], device_id=my_plane(dy, d, kk), device_id_type=MESH,
                )
                copy.start()
                sends.append(copy)
                back += 1
        if dy == 0:
            ret[k, here] = res[base + w_own * 2 + k]

    for dy, d in [(0, 0)] + plane_steps[::-1]:
        pos = lax.rem(y + dy, YS) * RING
        mine_at, other_at = pos + lax.rem(w_own + d, RING), pos + lax.rem(r_own + d, RING)
        if (dy, d) != (0, 0):
            landed(ret.at[k, mine_at], tr_sem.at[k, mine_at])
        landed(ret.at[1 - k, other_at], tr_sem.at[1 - k, other_at])

    lanes = out_ref.shape[3] // PLANE
    for pos in range(PLANE):
        for c in range(HALF):
            tile = ret[0, pos, c].astype(F32)
            for part in range(2):
                out_ref[part, c, :, pl.ds(pos * lanes, lanes)] = tile[part * NB:(part + 1) * NB]
    group = iota((2 * NB, lanes), 1) // (CORES * NB)
    for yy in range(YS):
        for c in range(HALF):
            tiles = [ret[1, yy * RING + i, c].astype(F32) for i in range(RING)]
            for bit in (1, 2, 4):
                high = (group // bit) % 2 == 1
                swapped = list(tiles)
                for i in range(RING):
                    if i & bit:
                        continue
                    a, b = tiles[i], tiles[i | bit]
                    shift = bit * CORES * NB
                    swapped[i] = jnp.where(high, pltpu.roll(b, shift, 1), a)
                    swapped[i | bit] = jnp.where(high, b, pltpu.roll(a, lanes - shift, 1))
                tiles = swapped
            for i in range(RING):
                for part in range(2):
                    out_ref[part, HALF + c, :, pl.ds((yy * RING + i) * lanes, lanes)] = (
                        tiles[i][part * NB:(part + 1) * NB]
                    )
    for copy in sends:
        copy.wait_send()


def body(voltages, weights):
    samples = voltages.shape[4]
    elems = voltages.shape[2]
    mine_ch = CH // PARTS
    devices = PLANE * RING * CORES
    volt = voltages.reshape(2 * elems * CH, samples)
    w = weights.reshape(2, NB * elems, CH)
    lanes = RING * CORES * NB
    gathers = 2 * (RING - 1) + 2 * (PLANE - 1) + 2
    return pl.pallas_call(
        functools.partial(kernel, 1.0 / samples),
        out_shape=jax.ShapeDtypeStruct((2, mine_ch, NB, devices * NB), F32),
        in_specs=[pl.BlockSpec(memory_space=pl.ANY)] * 2,
        out_specs=pl.BlockSpec(memory_space=pltpu.VMEM),
        scratch_shapes=[
            pltpu.VMEM(volt.shape, BF16),
            pltpu.VMEM(w.shape, BF16),
            pltpu.VMEM((CH * 2 * NB, samples), F32),
            pltpu.VMEM((CH * 2 * NB, samples), BF16),
            pltpu.VMEM((PARTS - 1, mine_ch * 2 * NB, samples), BF16),
            pltpu.VMEM((2, HALF, 2 * NB, samples), BF16),
            pltpu.VMEM((RING * CORES, HALF, 2 * NB, samples), BF16),
            pltpu.VMEM((PLANE * CORES, HALF, 2 * NB, samples), BF16),
            pltpu.VMEM((PLANE * CORES, HALF, 2 * NB, lanes), BF16),
            pltpu.VMEM((2, PLANE, HALF, 2 * NB, lanes), BF16),
            pltpu.SemaphoreType.DMA((2,)),
            pltpu.SemaphoreType.DMA((PARTS - 1,)),
            pltpu.SemaphoreType.DMA((PARTS - 1,)),
            pltpu.SemaphoreType.DMA((gathers,)),
            pltpu.SemaphoreType.DMA((RING * CORES,)),
            pltpu.SemaphoreType.DMA((PLANE * CORES,)),
            pltpu.SemaphoreType.DMA((PLANE * CORES,)),
            pltpu.SemaphoreType.DMA((2, PLANE)),
        ],
        compiler_params=pltpu.CompilerParams(collective_id=0, has_side_effects=True),
    )(volt, w)


def solution(mesh):
    placed = (P(None, "stn", "elem", None, None), P(None, None, "elem", None))
    return jax.shard_map(
        body, mesh=mesh, in_specs=placed, out_specs=P(None, "elem", "stn", None), check_vma=False
    )
```

```python
import functools

import jax
import jax.numpy as jnp
from jax import lax
from jax.experimental import pallas as pl
from jax.experimental.pallas import tpu as pltpu
from jax.sharding import PartitionSpec as P

MESH = pl.DeviceIdType.MESH
F32, BF16 = jnp.float32, jnp.bfloat16
RING, YS, CORES, PARTS = 8, 2, 2, 4
NB, CH, HALF = 8, 16, 2
FAR = (4, 3, 5, 2, 6, 1, 7)


def iota(shape, dim):
    return lax.broadcasted_iota(jnp.int32, shape, dim)


def beam_matrix(w_ref):
    elems = w_ref.shape[1] // NB
    spread = (iota((CH, elems * CH), 1) % CH == iota((CH, elems * CH), 0)).astype(F32).astype(BF16)
    shape = (NB * elems, elems * CH)
    own = iota(shape, 0) % elems == iota(shape, 1) // CH
    shape = (2 * NB, NB * elems)
    pick = (iota(shape, 0) % NB == iota(shape, 1) // elems).astype(F32).astype(BF16)
    flat = []
    for part in range(2):
        wide = jnp.dot(w_ref[part], spread, preferred_element_type=F32)
        wide = jnp.where(own, wide, 0.0).astype(BF16)
        flat.append(jnp.dot(pick, wide, preferred_element_type=F32))
    top = iota(flat[0].shape, 0) < NB
    left = jnp.where(top, flat[0], -flat[1])
    right = jnp.where(top, flat[1], flat[0])
    both = jnp.concatenate([left, right], axis=1)
    lane = iota(both.shape, 1) % CH
    return jnp.concatenate(
        [jnp.where(lane == c, both, 0.0).astype(BF16) for c in range(CH)], axis=0
    )


def kernel(scale, volt_hbm, w_hbm, ret, volt, w, part32, part16, got, mine, cols, rows, res,
           in_sem, es_sem, er_sem, gs_sem, cr_sem, rr_sem, ts_sem, tr_sem):
    s, e = lax.axis_index("stn"), lax.axis_index("elem")
    k, x = lax.rem(s, 2), lax.rem(s // 2, RING)
    z, y = lax.rem(s // (2 * RING), RING), s // (2 * RING * RING)
    r_own, w_own = x + k * (z - x), z + k * (x - z)

    def at(yy, rr, ww, kk):
        zz, xx = ww + k * (rr - ww), rr + k * (ww - rr)
        return {"stn": ((yy * RING + zz) * RING + xx) * 2 + kk, "elem": e}

    def along_r(dy, d, kk):
        return at(lax.rem(y + dy, YS), lax.rem(r_own + d, RING), w_own, kk)

    def along_w(dy, d, kk):
        return at(lax.rem(y + dy, YS), r_own, lax.rem(w_own + d, RING), kk)

    partner = at(y, r_own, w_own, 1 - k)

    barrier = pltpu.get_barrier_semaphore()
    peers = 0

    def greet(device):
        nonlocal peers
        pl.semaphore_signal(barrier, inc=1, device_id=device, device_id_type=MESH)
        peers += 1

    for d in (2, 1, 3):
        greet({"stn": s, "elem": lax.rem(e + d, PARTS)})
    for d in FAR:
        for dy in (1, 0):
            greet(along_r(dy, d, k))
            greet(along_r(dy, d, 1 - k))
            greet(along_w(dy, d, 1 - k))
        greet(along_w(0, d, k))
    greet(along_r(1, 0, k))
    greet(along_r(1, 0, 1 - k))
    greet(partner)

    load_v = pltpu.make_async_copy(volt_hbm, volt, in_sem.at[0])
    load_w = pltpu.make_async_copy(w_hbm, w, in_sem.at[1])
    load_w.start()
    load_v.start()
    load_w.wait()
    matrix = beam_matrix(w)
    load_v.wait()
    partial = jnp.dot(matrix, volt[...], preferred_element_type=F32)
    part32[...] = partial
    part16[...] = partial.astype(part16.dtype)
    pl.semaphore_wait(barrier, peers)

    quarter = part32.shape[0] // PARTS
    sends = []
    for d in (2, 1, 3):
        q = lax.rem(e + d, PARTS)
        copy = pltpu.make_async_remote_copy(
            src_ref=part16.at[pl.ds(pl.multiple_of(q * quarter, quarter), quarter)],
            dst_ref=got.at[d - 1],
            send_sem=es_sem.at[d - 1],
            recv_sem=er_sem.at[d - 1],
            device_id={"stn": s, "elem": q},
            device_id_type=MESH,
        )
        copy.start()
        sends.append(copy)
    total = part32[pl.ds(pl.multiple_of(e * quarter, quarter), quarter)]
    for copy in sends[::-1]:
        copy.wait_recv()
    for d in (1, 2, 3):
        total = total + got[d - 1].astype(F32)
    mine[...] = total.astype(BF16).reshape(mine.shape)

    count = 0

    def send(src, dst, sem, device):
        nonlocal count
        copy = pltpu.make_async_remote_copy(
            src_ref=src, dst_ref=dst, send_sem=gs_sem.at[count], recv_sem=sem,
            device_id=device, device_id_type=MESH,
        )
        copy.start()
        sends.append(copy)
        count += 1

    col, row = r_own * 2 + k, w_own * 2 + k
    other_col, other_row = w_own * 2 + k, r_own * 2 + k
    own, other = mine.at[k], mine.at[1 - k]
    for d in FAR:
        send(own, cols.at[y, col], cr_sem.at[y, col], along_r(0, d, k))
        send(other, cols.at[y, other_col], cr_sem.at[y, other_col], along_w(0, d, 1 - k))
    for d in FAR:
        send(own, rows.at[row], rr_sem.at[row], along_w(0, d, k))
        send(other, rows.at[other_row], rr_sem.at[other_row], along_r(0, d, 1 - k))
    for d in FAR + (0,):
        send(own, cols.at[y, col], cr_sem.at[y, col], along_r(1, d, k))
        send(other, cols.at[y, other_col], cr_sem.at[y, other_col], along_w(1, d, 1 - k))
    send(other, cols.at[y, other_col], cr_sem.at[y, other_col], partner)
    send(other, rows.at[other_row], rr_sem.at[other_row], partner)
    half = mine[k]
    cols[y, col] = half
    rows[row] = half

    def landed(dst, sem):
        pltpu.make_async_remote_copy(
            src_ref=dst, dst_ref=dst, send_sem=gs_sem.at[0], recv_sem=sem,
            device_id=partner, device_id_type=MESH,
        ).wait_recv()

    def rows_landed():
        landed(rows.at[w_own * 2 + 1 - k], rr_sem.at[w_own * 2 + 1 - k])
        for d in FAR[::-1]:
            for kk in range(2):
                slot = lax.rem(w_own + d, RING) * 2 + kk
                landed(rows.at[slot], rr_sem.at[slot])

    cross = (((1,), (1,)), ((), ()))
    back = 0
    turned = [None] * HALF
    for dy in range(YS):
        yy = lax.rem(y + dy, YS)
        for d in (0,) + FAR[::-1]:
            base = lax.rem(r_own + d, RING) * 2
            for slot in (base + 1 - k,) if (dy, d) == (0, 0) else (base, base + 1):
                landed(cols.at[yy, slot], cr_sem.at[yy, slot])
        if dy == 0:
            rows_landed()
        for c in range(HALF):
            tile = rows[:, c]
            n, _, samples = tile.shape
            if dy == 0:
                wide = tile.astype(F32).reshape(n, 2, NB, samples)
                wide = jnp.concatenate([wide[:, 1:], -wide[:, :1]], axis=1)
                turned[c] = wide.reshape(n * 2 * NB, samples).astype(BF16)
            wide = cols[yy, :, c].astype(F32).reshape(RING * CORES, 2, NB, samples)
            real, imag = (wide[:, p].reshape(RING * CORES * NB, samples).astype(BF16) for p in range(2))
            prod = lax.dot_general(tile.reshape(n * 2 * NB, samples), real, cross, preferred_element_type=F32)
            prod += lax.dot_general(turned[c], imag, cross, preferred_element_type=F32)
            res[yy, :, c] = (prod * scale).astype(BF16).reshape(n, 2 * NB, -1)
        for d in FAR + (0,):
            slot = lax.rem(w_own + d, RING) * 2
            for kk in (1 - k,) if d == 0 else (0, 1):
                copy = pltpu.make_async_remote_copy(
                    src_ref=res.at[yy, slot + kk], dst_ref=ret.at[k, yy, w_own], send_sem=ts_sem.at[back],
                    recv_sem=tr_sem.at[k, yy, w_own], device_id=along_w(0, d, kk), device_id_type=MESH,
                )
                copy.start()
                sends.append(copy)
                back += 1
        ret[k, yy, w_own] = res[yy, row]

    for dy in range(YS):
        yy = lax.rem(y + dy, YS)
        for d in (0,) + FAR[::-1]:
            if d:
                slot = lax.rem(w_own + d, RING)
                landed(ret.at[k, yy, slot], tr_sem.at[k, yy, slot])
            slot = lax.rem(r_own + d, RING)
            landed(ret.at[1 - k, yy, slot], tr_sem.at[1 - k, yy, slot])
    for copy in sends:
        copy.wait_send()


def unpack(ret, out_hbm, out, sem):
    lanes = ret.shape[-1]
    group = iota((2 * NB, lanes), 1) // (CORES * NB)
    copies = []
    for h in range(2):
        for c in range(HALF):
            for yy in range(YS):
                tiles = [ret[h, yy, i, c].astype(F32) for i in range(RING)]
                for bit in (1, 2, 4) if h else ():
                    high = (group // bit) % 2 == 1
                    swapped = list(tiles)
                    for i in range(RING):
                        if i & bit:
                            continue
                        a, b = tiles[i], tiles[i | bit]
                        shift = bit * CORES * NB
                        swapped[i] = jnp.where(high, pltpu.roll(b, shift, 1), a)
                        swapped[i | bit] = jnp.where(high, b, pltpu.roll(a, lanes - shift, 1))
                    tiles = swapped
                for i in range(RING):
                    where = pl.ds((yy * RING + i) * lanes, lanes)
                    for part in range(2):
                        out[part, h * HALF + c, :, where] = tiles[i][part * NB:(part + 1) * NB]
            for part in range(2):
                ch = h * HALF + c
                copy = pltpu.make_async_copy(out.at[part, ch], out_hbm.at[part, ch], sem.at[part, ch])
                copy.start()
                copies.append(copy)
    for copy in copies:
        copy.wait()


def body(voltages, weights):
    samples = voltages.shape[4]
    elems = voltages.shape[2]
    mine_ch = CH // PARTS
    volt = voltages.reshape(2 * elems * CH, samples)
    w = weights.reshape(2, NB * elems, CH)
    lanes = RING * CORES * NB
    block = (HALF, 2 * NB, samples)
    result = (HALF, 2 * NB, lanes)
    gathers = 4 * (RING - 1) + 2 * RING + 2
    dma = pltpu.SemaphoreType.DMA
    ret = pl.pallas_call(
        functools.partial(kernel, 1.0 / samples),
        out_shape=pltpu.VMEM((2, YS, RING) + result, BF16),
        in_specs=[pl.BlockSpec(memory_space=pl.ANY)] * 2,
        out_specs=pl.BlockSpec(memory_space=pltpu.VMEM),
        scratch_shapes=[
            pltpu.VMEM(volt.shape, BF16),
            pltpu.VMEM(w.shape, BF16),
            pltpu.VMEM((CH * 2 * NB, samples), F32),
            pltpu.VMEM((CH * 2 * NB, samples), BF16),
            pltpu.VMEM((PARTS - 1, mine_ch * 2 * NB, samples), BF16),
            pltpu.VMEM((2,) + block, BF16),
            pltpu.VMEM((YS, RING * CORES) + block, BF16),
            pltpu.VMEM((RING * CORES,) + block, BF16),
            pltpu.VMEM((YS, RING * CORES) + result, BF16),
            dma((2,)),
            dma((PARTS - 1,)),
            dma((PARTS - 1,)),
            dma((gathers,)),
            dma((YS, RING * CORES)),
            dma((RING * CORES,)),
            dma((YS * RING * CORES,)),
            dma((2, YS, RING)),
        ],
        compiler_params=pltpu.CompilerParams(collective_id=0, has_side_effects=True),
    )(volt, w)
    shape = (2, mine_ch, NB, YS * RING * lanes)
    return pl.pallas_call(
        unpack,
        out_shape=jax.ShapeDtypeStruct(shape, F32),
        in_specs=[pl.BlockSpec(memory_space=pltpu.VMEM)],
        out_specs=pl.BlockSpec(memory_space=pl.ANY),
        scratch_shapes=[pltpu.VMEM(shape, F32), dma((2, mine_ch))],
    )(pltpu.with_memory_space_constraint(ret, pltpu.VMEM))


def solution(mesh):
    placed = (P(None, "stn", "elem", None, None), P(None, None, "elem", None))
    return jax.shard_map(
        body, mesh=mesh, in_specs=placed, out_specs=P(None, "elem", "stn", None), check_vma=False
    )
```

```python
import functools

import jax
import jax.numpy as jnp
from jax import lax
from jax.experimental import pallas as pl
from jax.experimental.pallas import tpu as pltpu
from jax.sharding import PartitionSpec as P

MESH = pl.DeviceIdType.MESH
F32, BF16 = jnp.float32, jnp.bfloat16
RING, YS, CORES, PARTS = 8, 2, 2, 4
NB, CH, HALF = 8, 16, 2
FAR = (4, 3, 5, 2, 6, 1, 7)


def iota(shape, dim):
    return lax.broadcasted_iota(jnp.int32, shape, dim)


def beam_matrix(w_ref):
    elems = w_ref.shape[1] // NB
    spread = (iota((CH, elems * CH), 1) % CH == iota((CH, elems * CH), 0)).astype(F32).astype(BF16)
    shape = (NB * elems, elems * CH)
    own = iota(shape, 0) % elems == iota(shape, 1) // CH
    shape = (2 * NB, NB * elems)
    pick = (iota(shape, 0) % NB == iota(shape, 1) // elems).astype(F32).astype(BF16)
    flat = []
    for part in range(2):
        wide = jnp.dot(w_ref[part], spread, preferred_element_type=F32)
        wide = jnp.where(own, wide, 0.0).astype(BF16)
        flat.append(jnp.dot(pick, wide, preferred_element_type=F32))
    top = iota(flat[0].shape, 0) < NB
    left = jnp.where(top, flat[0], -flat[1])
    right = jnp.where(top, flat[1], flat[0])
    both = jnp.concatenate([left, right], axis=1)
    lane = iota(both.shape, 1) % CH
    return jnp.concatenate(
        [jnp.where(lane == c, both, 0.0).astype(BF16) for c in range(CH)], axis=0
    )


def kernel(scale, volt_hbm, w_hbm, ret, early, volt, w, part32, part16, got, mine, cols, rows, res,
           in_sem, es_sem, er_sem, gs_sem, cr_sem, rr_sem, ts_sem, tr_sem):
    s, e = lax.axis_index("stn"), lax.axis_index("elem")
    k, x = lax.rem(s, 2), lax.rem(s // 2, RING)
    z, y = lax.rem(s // (2 * RING), RING), s // (2 * RING * RING)
    r_own, w_own = x + k * (z - x), z + k * (x - z)

    def at(yy, rr, ww, kk):
        zz, xx = ww + k * (rr - ww), rr + k * (ww - rr)
        return {"stn": ((yy * RING + zz) * RING + xx) * 2 + kk, "elem": e}

    def along_r(dy, d, kk):
        return at(lax.rem(y + dy, YS), lax.rem(r_own + d, RING), w_own, kk)

    def along_w(dy, d, kk):
        return at(lax.rem(y + dy, YS), r_own, lax.rem(w_own + d, RING), kk)

    partner = at(y, r_own, w_own, 1 - k)

    load_v = pltpu.make_async_copy(volt_hbm, volt, in_sem.at[0])
    load_w = pltpu.make_async_copy(w_hbm, w, in_sem.at[1])
    load_w.start()
    load_v.start()

    barrier = pltpu.get_barrier_semaphore()
    peers = 0

    def greet(device):
        nonlocal peers
        pl.semaphore_signal(barrier, inc=1, device_id=device, device_id_type=MESH)
        peers += 1

    for d in (2, 1, 3):
        greet({"stn": s, "elem": lax.rem(e + d, PARTS)})
    for d in FAR:
        for dy in (1, 0):
            greet(along_r(dy, d, k))
            greet(along_r(dy, d, 1 - k))
            greet(along_w(dy, d, 1 - k))
        greet(along_w(0, d, k))
    greet(along_r(1, 0, k))
    greet(along_r(1, 0, 1 - k))
    greet(partner)

    load_w.wait()
    matrix = beam_matrix(w)
    load_v.wait()
    partial = jnp.dot(matrix, volt[...], preferred_element_type=F32)
    part32[...] = partial
    part16[...] = partial.astype(part16.dtype)
    pl.semaphore_wait(barrier, peers)

    quarter = part32.shape[0] // PARTS
    piece = quarter // 2

    def rows_of(q, h):
        return pl.ds(pl.multiple_of(q * quarter + h * piece, piece), piece)

    sends, partials = [], ([], [])
    for turn, h in enumerate((k, 1 - k)):
        for d in (2, 1, 3):
            q = lax.rem(e + d, PARTS)
            copy = pltpu.make_async_remote_copy(
                src_ref=part16.at[rows_of(q, h)],
                dst_ref=got.at[d - 1, turn],
                send_sem=es_sem.at[d - 1, turn],
                recv_sem=er_sem.at[d - 1, turn],
                device_id={"stn": s, "elem": q},
                device_id_type=MESH,
            )
            copy.start()
            sends.append(copy)
            partials[turn].append(copy)

    def add_up(turn, h):
        total = part32[rows_of(e, h)]
        for copy in partials[turn][::-1]:
            copy.wait_recv()
        for d in (1, 2, 3):
            total = total + got[d - 1, turn].astype(F32)
        mine[h] = total.astype(BF16).reshape(mine.shape[1:])

    count = 0

    def send(src, dst, sem, device):
        nonlocal count
        copy = pltpu.make_async_remote_copy(
            src_ref=src, dst_ref=dst, send_sem=gs_sem.at[count], recv_sem=sem,
            device_id=device, device_id_type=MESH,
        )
        copy.start()
        sends.append(copy)
        count += 1

    col, row = r_own * 2 + k, w_own * 2 + k
    other_col, other_row = w_own * 2 + k, r_own * 2 + k
    own, other = mine.at[k], mine.at[1 - k]
    add_up(0, k)
    for d in FAR:
        send(own, cols.at[y, col], cr_sem.at[y, col], along_r(1, d, k))
    for d in FAR:
        send(own, rows.at[row], rr_sem.at[row], along_w(0, d, k))
    for d in FAR:
        send(own, cols.at[y, col], cr_sem.at[y, col], along_r(0, d, k))
    send(own, cols.at[y, col], cr_sem.at[y, col], along_r(1, 0, k))
    add_up(1, 1 - k)
    for d in FAR:
        send(other, cols.at[y, other_col], cr_sem.at[y, other_col], along_w(1, d, 1 - k))
    for d in FAR:
        send(other, rows.at[other_row], rr_sem.at[other_row], along_r(0, d, 1 - k))
    for d in FAR:
        send(other, cols.at[y, other_col], cr_sem.at[y, other_col], along_w(0, d, 1 - k))
    send(other, cols.at[y, other_col], cr_sem.at[y, other_col], along_w(1, 0, 1 - k))
    send(other, cols.at[y, other_col], cr_sem.at[y, other_col], partner)
    send(other, rows.at[other_row], rr_sem.at[other_row], partner)
    half = mine[k]
    cols[y, col] = half
    rows[row] = half

    def landed(dst, sem):
        pltpu.make_async_remote_copy(
            src_ref=dst, dst_ref=dst, send_sem=gs_sem.at[0], recv_sem=sem,
            device_id=partner, device_id_type=MESH,
        ).wait_recv()

    def rows_landed():
        landed(rows.at[w_own * 2 + 1 - k], rr_sem.at[w_own * 2 + 1 - k])
        for d in FAR[::-1]:
            for kk in range(2):
                slot = lax.rem(w_own + d, RING) * 2 + kk
                landed(rows.at[slot], rr_sem.at[slot])

    cross = (((1,), (1,)), ((), ()))
    back = 0
    turned = [None] * HALF
    for dy in (1, 0):
        yy = lax.rem(y + dy, YS)
        for d in (0,) + FAR[::-1]:
            base = lax.rem(r_own + d, RING) * 2
            for slot in (base + 1 - k,) if (dy, d) == (0, 0) else (base, base + 1):
                landed(cols.at[yy, slot], cr_sem.at[yy, slot])
        if dy == 1:
            rows_landed()
        for c in range(HALF):
            tile = rows[:, c]
            n, _, samples = tile.shape
            if dy == 1:
                wide = tile.astype(F32).reshape(n, 2, NB, samples)
                wide = jnp.concatenate([wide[:, 1:], -wide[:, :1]], axis=1)
                turned[c] = wide.reshape(n * 2 * NB, samples).astype(BF16)
            wide = cols[yy, :, c].astype(F32).reshape(RING * CORES, 2, NB, samples)
            real, imag = (wide[:, p].reshape(RING * CORES * NB, samples).astype(BF16) for p in range(2))
            prod = lax.dot_general(tile.reshape(n * 2 * NB, samples), real, cross, preferred_element_type=F32)
            prod += lax.dot_general(turned[c], imag, cross, preferred_element_type=F32)
            res[yy, :, c] = (prod * scale).astype(BF16).reshape(n, 2 * NB, -1)
        for d in FAR + (0,):
            slot = lax.rem(w_own + d, RING) * 2
            for kk in (1 - k,) if d == 0 else (0, 1):
                copy = pltpu.make_async_remote_copy(
                    src_ref=res.at[yy, slot + kk], dst_ref=ret.at[k, yy, w_own], send_sem=ts_sem.at[back],
                    recv_sem=tr_sem.at[k, yy, w_own], device_id=along_w(0, d, kk), device_id_type=MESH,
                )
                copy.start()
                sends.append(copy)
                back += 1
        ret[k, yy, w_own] = res[yy, row]

    for copy in sends:
        copy.wait_send()

    for dy in (1, 0):
        yy = lax.rem(y + dy, YS)
        for d in (0,) + FAR[::-1]:
            if d:
                slot = lax.rem(w_own + d, RING)
                landed(ret.at[k, yy, slot], tr_sem.at[k, yy, slot])
            slot = lax.rem(r_own + d, RING)
            landed(ret.at[1 - k, yy, slot], tr_sem.at[1 - k, yy, slot])
        if dy == 1:
            unpack(ret, early, yy)


def unpack(ret, out, yy):
    lanes = ret.shape[-1]
    group = iota((2 * NB, lanes), 1) // (CORES * NB)
    for h in range(2):
        for c in range(HALF):
            tiles = [ret[h, yy, i, c].astype(F32) for i in range(RING)]
            for bit in (1, 2, 4) if h else ():
                high = (group // bit) % 2 == 1
                swapped = list(tiles)
                for i in range(RING):
                    if i & bit:
                        continue
                    a, b = tiles[i], tiles[i | bit]
                    shift = bit * CORES * NB
                    swapped[i] = jnp.where(high, pltpu.roll(b, shift, 1), a)
                    swapped[i | bit] = jnp.where(high, b, pltpu.roll(a, lanes - shift, 1))
                tiles = swapped
            for i in range(RING):
                for part in range(2):
                    out[part, h * HALF + c, :, pl.ds(i * lanes, lanes)] = tiles[i][part * NB:(part + 1) * NB]


def place(out_hbm, yy):
    width = out_hbm.shape[3] // YS
    return out_hbm.at[:, :, :, pl.ds(pl.multiple_of(yy * width, width), width)]


def finish(ret, early, out_hbm, out, sem):
    y = lax.axis_index("stn") // (2 * RING * RING)
    first = pltpu.make_async_copy(early, place(out_hbm, 1 - y), sem.at[0])
    first.start()
    unpack(ret, out, y)
    last = pltpu.make_async_copy(out, place(out_hbm, y), sem.at[1])
    last.start()
    first.wait()
    last.wait()


def body(voltages, weights):
    samples = voltages.shape[4]
    elems = voltages.shape[2]
    mine_ch = CH // PARTS
    volt = voltages.reshape(2 * elems * CH, samples)
    w = weights.reshape(2, NB * elems, CH)
    lanes = RING * CORES * NB
    block = (HALF, 2 * NB, samples)
    result = (HALF, 2 * NB, lanes)
    gathers = 4 * (RING - 1) + 2 * RING + 2
    dma = pltpu.SemaphoreType.DMA
    shape = (2, mine_ch, NB, YS * RING * lanes)
    half = shape[:3] + (RING * lanes,)
    ret, early = pl.pallas_call(
        functools.partial(kernel, 1.0 / samples),
        out_shape=(pltpu.VMEM((2, YS, RING) + result, BF16), pltpu.VMEM(half, F32)),
        in_specs=[pl.BlockSpec(memory_space=pl.ANY)] * 2,
        out_specs=(pl.BlockSpec(memory_space=pltpu.VMEM),) * 2,
        scratch_shapes=[
            pltpu.VMEM(volt.shape, BF16),
            pltpu.VMEM(w.shape, BF16),
            pltpu.VMEM((CH * 2 * NB, samples), F32),
            pltpu.VMEM((CH * 2 * NB, samples), BF16),
            pltpu.VMEM((PARTS - 1, 2, HALF * 2 * NB, samples), BF16),
            pltpu.VMEM((2,) + block, BF16),
            pltpu.VMEM((YS, RING * CORES) + block, BF16),
            pltpu.VMEM((RING * CORES,) + block, BF16),
            pltpu.VMEM((YS, RING * CORES) + result, BF16),
            dma((2,)),
            dma((PARTS - 1, 2)),
            dma((PARTS - 1, 2)),
            dma((gathers,)),
            dma((YS, RING * CORES)),
            dma((RING * CORES,)),
            dma((YS * RING * CORES,)),
            dma((2, YS, RING)),
        ],
        compiler_params=pltpu.CompilerParams(collective_id=0, has_side_effects=True),
    )(volt, w)
    return pl.pallas_call(
        finish,
        out_shape=jax.ShapeDtypeStruct(shape, F32),
        in_specs=[pl.BlockSpec(memory_space=pltpu.VMEM)] * 2,
        out_specs=pl.BlockSpec(memory_space=pl.ANY),
        scratch_shapes=[pltpu.VMEM(half, F32), dma((2,))],
    )(*(pltpu.with_memory_space_constraint(a, pltpu.VMEM) for a in (ret, early)))


def solution(mesh):
    placed = (P(None, "stn", "elem", None, None), P(None, None, "elem", None))
    return jax.shard_map(
        body, mesh=mesh, in_specs=placed, out_specs=P(None, "elem", "stn", None), check_vma=False
    )
```

```python
import functools

import jax
import jax.numpy as jnp
from jax import lax
from jax.experimental import pallas as pl
from jax.experimental.pallas import tpu as pltpu
from jax.sharding import PartitionSpec as P

MESH = pl.DeviceIdType.MESH
F32, BF16 = jnp.float32, jnp.bfloat16
RING, YS, CORES, PARTS = 8, 2, 2, 4
NB, CH, HALF = 8, 16, 2
FAR = (4, 3, 5, 2, 6, 1, 7)


def iota(shape, dim):
    return lax.broadcasted_iota(jnp.int32, shape, dim)


def beam_matrix(w_ref):
    elems = w_ref.shape[1] // NB
    spread = (iota((CH, elems * CH), 1) % CH == iota((CH, elems * CH), 0)).astype(F32).astype(BF16)
    shape = (NB * elems, elems * CH)
    own = iota(shape, 0) % elems == iota(shape, 1) // CH
    shape = (2 * NB, NB * elems)
    pick = (iota(shape, 0) % NB == iota(shape, 1) // elems).astype(F32).astype(BF16)
    flat = []
    for part in range(2):
        wide = jnp.dot(w_ref[part], spread, preferred_element_type=F32)
        wide = jnp.where(own, wide, 0.0).astype(BF16)
        flat.append(jnp.dot(pick, wide, preferred_element_type=F32))
    top = iota(flat[0].shape, 0) < NB
    left = jnp.where(top, flat[0], -flat[1])
    right = jnp.where(top, flat[1], flat[0])
    both = jnp.concatenate([left, right], axis=1)
    lane = iota(both.shape, 1) % CH
    return jnp.concatenate(
        [jnp.where(lane == c, both, 0.0).astype(BF16) for c in range(CH)], axis=0
    )


def kernel(scale, volt_hbm, w_hbm, ret, early, volt, w, part32, part16, got, mine, cols, rows, res,
           in_sem, es_sem, er_sem, gs_sem, cr_sem, rr_sem, ts_sem, tr_sem, here, zs_sem):
    s, e = lax.axis_index("stn"), lax.axis_index("elem")
    k, x = lax.rem(s, 2), lax.rem(s // 2, RING)
    z, y = lax.rem(s // (2 * RING), RING), s // (2 * RING * RING)
    r_own, w_own = x + k * (z - x), z + k * (x - z)

    def at(yy, rr, ww, kk):
        zz, xx = ww + k * (rr - ww), rr + k * (ww - rr)
        return {"stn": ((yy * RING + zz) * RING + xx) * 2 + kk, "elem": e}

    def along_r(dy, d, kk):
        return at(lax.rem(y + dy, YS), lax.rem(r_own + d, RING), w_own, kk)

    def along_w(dy, d, kk):
        return at(lax.rem(y + dy, YS), r_own, lax.rem(w_own + d, RING), kk)

    partner = at(y, r_own, w_own, 1 - k)
    facing = at(1 - y, r_own, w_own, k)

    load_v = pltpu.make_async_copy(volt_hbm, volt, in_sem.at[0])
    load_w = pltpu.make_async_copy(w_hbm, w, in_sem.at[1])
    load_w.start()
    load_v.start()

    def device(zz, xx, kk):
        return {"stn": ((y * RING + zz) * RING + xx) * 2 + kk, "elem": e}

    barrier = pltpu.get_barrier_semaphore()
    peers = 0

    def greet(peer):
        nonlocal peers
        pl.semaphore_signal(barrier, inc=1, device_id=peer, device_id_type=MESH)
        peers += 1

    for d in (2, 1, 3):
        greet({"stn": s, "elem": lax.rem(e + d, PARTS)})
    for d in FAR:
        for kk in range(CORES):
            greet(device(z, lax.rem(x + d, RING), kk))
    greet(facing)
    greet(partner)
    for zz in range(1, RING):
        @pl.when(zz > z)
        def _():
            for kk in range(CORES):
                pl.semaphore_signal(barrier, inc=1, device_id=device(zz, x, kk), device_id_type=MESH)

    load_w.wait()
    matrix = beam_matrix(w)
    load_v.wait()
    partial = jnp.dot(matrix, volt[...], preferred_element_type=F32)
    part32[...] = partial
    part16[...] = partial.astype(part16.dtype)
    pl.semaphore_wait(barrier, peers + CORES * z)
    for zz in range(RING - 1):
        @pl.when(zz < z)
        def _():
            for kk in range(CORES):
                pl.semaphore_signal(here.at[z], inc=1, device_id=device(zz, x, kk), device_id_type=MESH)

    quarter = part32.shape[0] // PARTS
    piece = quarter // 2

    def rows_of(q, h):
        return pl.ds(pl.multiple_of(q * quarter + h * piece, piece), piece)

    sends, partials = [], ([], [])
    for turn, h in enumerate((k, 1 - k)):
        for d in (2, 1, 3):
            q = lax.rem(e + d, PARTS)
            copy = pltpu.make_async_remote_copy(
                src_ref=part16.at[rows_of(q, h)],
                dst_ref=got.at[d - 1, turn],
                send_sem=es_sem.at[d - 1, turn],
                recv_sem=er_sem.at[d - 1, turn],
                device_id={"stn": s, "elem": q},
                device_id_type=MESH,
            )
            copy.start()
            sends.append(copy)
            partials[turn].append(copy)

    def add_up(turn, h):
        total = part32[rows_of(e, h)]
        for copy in partials[turn][::-1]:
            copy.wait_recv()
        for d in (1, 2, 3):
            total = total + got[d - 1, turn].astype(F32)
        mine[h] = total.astype(BF16).reshape(mine.shape[1:])

    count = 0

    def send(src, dst, sem, device):
        nonlocal count
        copy = pltpu.make_async_remote_copy(
            src_ref=src, dst_ref=dst, send_sem=gs_sem.at[count], recv_sem=sem,
            device_id=device, device_id_type=MESH,
        )
        copy.start()
        sends.append(copy)
        count += 1

    col, row = r_own * 2 + k, w_own * 2 + k
    other_col, other_row = w_own * 2 + k, r_own * 2 + k
    add_up(0, k)
    add_up(1, 1 - k)
    for d in FAR:
        xx = lax.rem(x + d, RING)
        send(mine.at[0], cols.at[y, x * 2 + k], cr_sem.at[y, x * 2 + k], device(z, xx, 0))
    for d in FAR:
        xx = lax.rem(x + d, RING)
        send(mine.at[1], rows.at[x * 2 + k], rr_sem.at[x * 2 + k], device(z, xx, 1))
    other = mine.at[1 - k]
    send(other, cols.at[y, other_col], cr_sem.at[y, other_col], partner)
    send(other, rows.at[other_row], rr_sem.at[other_row], partner)

    def to_plane(zz):
        slot = z * 2 + k
        return [
            pltpu.make_async_remote_copy(
                src_ref=mine.at[1 - h], dst_ref=dst, send_sem=zs_sem.at[zz, h], recv_sem=sem,
                device_id=device(zz, x, 1 - h), device_id_type=MESH,
            )
            for h, (dst, sem) in enumerate(((cols.at[y, slot], cr_sem.at[y, slot]), (rows.at[slot], rr_sem.at[slot])))
        ]

    for zz in range(RING):
        @pl.when(zz > z)
        def _():
            pl.semaphore_wait(here.at[zz], CORES)

        @pl.when(zz != z)
        def _():
            for copy in to_plane(zz):
                copy.start()
    half = mine[k]
    cols[y, col] = half
    rows[row] = half

    def landed(dst, sem):
        pltpu.make_async_remote_copy(
            src_ref=dst, dst_ref=dst, send_sem=gs_sem.at[0], recv_sem=sem,
            device_id=partner, device_id_type=MESH,
        ).wait_recv()

    def rows_landed():
        landed(rows.at[w_own * 2 + 1 - k], rr_sem.at[w_own * 2 + 1 - k])
        for d in FAR[::-1]:
            for kk in range(2):
                slot = lax.rem(w_own + d, RING) * 2 + kk
                landed(rows.at[slot], rr_sem.at[slot])

    cross = (((1,), (1,)), ((), ()))
    back = 0
    turned = [None] * HALF
    for rr in range(RING):
        base = rr * 2

        @pl.when(rr != r_own)
        def _():
            for slot in (base, base + 1):
                landed(cols.at[y, slot], cr_sem.at[y, slot])

        @pl.when(rr == r_own)
        def _():
            landed(cols.at[y, base + 1 - k], cr_sem.at[y, base + 1 - k])

        pair = cols.at[y, pl.ds(base, 2)]
        send(pair, pair, cr_sem.at[y, base], facing)
    rows_landed()
    for dy in range(YS):
        yy = lax.rem(y + dy, YS)
        if dy == 1:
            for base in range(0, 2 * RING, 2):
                landed(cols.at[yy, pl.ds(base, 2)], cr_sem.at[yy, base])
        for c in range(HALF):
            tile = rows[:, c]
            n, _, samples = tile.shape
            if dy == 0:
                wide = tile.astype(F32).reshape(n, 2, NB, samples)
                wide = jnp.concatenate([wide[:, 1:], -wide[:, :1]], axis=1)
                turned[c] = wide.reshape(n * 2 * NB, samples).astype(BF16)
            wide = cols[yy, :, c].astype(F32).reshape(RING * CORES, 2, NB, samples)
            real, imag = (wide[:, p].reshape(RING * CORES * NB, samples).astype(BF16) for p in range(2))
            prod = lax.dot_general(tile.reshape(n * 2 * NB, samples), real, cross, preferred_element_type=F32)
            prod += lax.dot_general(turned[c], imag, cross, preferred_element_type=F32)
            res[yy, :, c] = (prod * scale).astype(BF16).reshape(n, 2 * NB, -1)
        for d in FAR + (0,):
            slot = lax.rem(w_own + d, RING) * 2
            for kk in (1 - k,) if d == 0 else (0, 1):
                copy = pltpu.make_async_remote_copy(
                    src_ref=res.at[yy, slot + kk], dst_ref=ret.at[k, yy, w_own], send_sem=ts_sem.at[back],
                    recv_sem=tr_sem.at[k, yy, w_own], device_id=along_w(0, d, kk), device_id_type=MESH,
                )
                copy.start()
                sends.append(copy)
                back += 1
        ret[k, yy, w_own] = res[yy, row]

    for copy in sends:
        copy.wait_send()
    for zz in range(RING):
        @pl.when(zz != z)
        def _():
            for copy in to_plane(zz):
                copy.wait_send()

    for dy in range(YS):
        yy = lax.rem(y + dy, YS)
        for d in (0,) + FAR[::-1]:
            if d:
                slot = lax.rem(w_own + d, RING)
                landed(ret.at[k, yy, slot], tr_sem.at[k, yy, slot])
            slot = lax.rem(r_own + d, RING)
            landed(ret.at[1 - k, yy, slot], tr_sem.at[1 - k, yy, slot])
        if dy == 0:
            unpack(ret, early, yy)


def unpack(ret, out, yy):
    lanes = ret.shape[-1]
    group = iota((2 * NB, lanes), 1) // (CORES * NB)
    for h in range(2):
        for c in range(HALF):
            tiles = [ret[h, yy, i, c].astype(F32) for i in range(RING)]
            for bit in (1, 2, 4) if h else ():
                high = (group // bit) % 2 == 1
                swapped = list(tiles)
                for i in range(RING):
                    if i & bit:
                        continue
                    a, b = tiles[i], tiles[i | bit]
                    shift = bit * CORES * NB
                    swapped[i] = jnp.where(high, pltpu.roll(b, shift, 1), a)
                    swapped[i | bit] = jnp.where(high, b, pltpu.roll(a, lanes - shift, 1))
                tiles = swapped
            for i in range(RING):
                for part in range(2):
                    out[part, h * HALF + c, :, pl.ds(i * lanes, lanes)] = tiles[i][part * NB:(part + 1) * NB]


def place(out_hbm, yy):
    width = out_hbm.shape[3] // YS
    return out_hbm.at[:, :, :, pl.ds(pl.multiple_of(yy * width, width), width)]


def finish(ret, early, out_hbm, out, sem):
    y = lax.axis_index("stn") // (2 * RING * RING)
    first = pltpu.make_async_copy(early, place(out_hbm, y), sem.at[0])
    first.start()
    unpack(ret, out, 1 - y)
    last = pltpu.make_async_copy(out, place(out_hbm, 1 - y), sem.at[1])
    last.start()
    first.wait()
    last.wait()


def body(voltages, weights):
    samples = voltages.shape[4]
    elems = voltages.shape[2]
    mine_ch = CH // PARTS
    volt = voltages.reshape(2 * elems * CH, samples)
    w = weights.reshape(2, NB * elems, CH)
    lanes = RING * CORES * NB
    block = (HALF, 2 * NB, samples)
    result = (HALF, 2 * NB, lanes)
    gathers = 2 * (RING - 1) + RING + 2
    dma = pltpu.SemaphoreType.DMA
    shape = (2, mine_ch, NB, YS * RING * lanes)
    half = shape[:3] + (RING * lanes,)
    ret, early = pl.pallas_call(
        functools.partial(kernel, 1.0 / samples),
        out_shape=(pltpu.VMEM((2, YS, RING) + result, BF16), pltpu.VMEM(half, F32)),
        in_specs=[pl.BlockSpec(memory_space=pl.ANY)] * 2,
        out_specs=(pl.BlockSpec(memory_space=pltpu.VMEM),) * 2,
        scratch_shapes=[
            pltpu.VMEM(volt.shape, BF16),
            pltpu.VMEM(w.shape, BF16),
            pltpu.VMEM((CH * 2 * NB, samples), F32),
            pltpu.VMEM((CH * 2 * NB, samples), BF16),
            pltpu.VMEM((PARTS - 1, 2, HALF * 2 * NB, samples), BF16),
            pltpu.VMEM((2,) + block, BF16),
            pltpu.VMEM((YS, RING * CORES) + block, BF16),
            pltpu.VMEM((RING * CORES,) + block, BF16),
            pltpu.VMEM((YS, RING * CORES) + result, BF16),
            dma((2,)),
            dma((PARTS - 1, 2)),
            dma((PARTS - 1, 2)),
            dma((gathers,)),
            dma((YS, RING * CORES)),
            dma((RING * CORES,)),
            dma((YS * RING * CORES,)),
            dma((2, YS, RING)),
            pltpu.SemaphoreType.REGULAR((RING,)),
            dma((RING, 2)),
        ],
        compiler_params=pltpu.CompilerParams(collective_id=0, has_side_effects=True),
    )(volt, w)
    return pl.pallas_call(
        finish,
        out_shape=jax.ShapeDtypeStruct(shape, F32),
        in_specs=[pl.BlockSpec(memory_space=pltpu.VMEM)] * 2,
        out_specs=pl.BlockSpec(memory_space=pl.ANY),
        scratch_shapes=[pltpu.VMEM(half, F32), dma((2,))],
    )(*(pltpu.with_memory_space_constraint(a, pltpu.VMEM) for a in (ret, early)))


def solution(mesh):
    placed = (P(None, "stn", "elem", None, None), P(None, None, "elem", None))
    return jax.shard_map(
        body, mesh=mesh, in_specs=placed, out_specs=P(None, "elem", "stn", None), check_vma=False
    )
```

```python
import functools

import jax
import jax.numpy as jnp
from jax import lax
from jax.experimental import pallas as pl
from jax.experimental.pallas import tpu as pltpu
from jax.sharding import PartitionSpec as P

MESH = pl.DeviceIdType.MESH
F32, BF16 = jnp.float32, jnp.bfloat16
RING, YS, CORES, PARTS = 8, 2, 2, 4
NB, CH, HALF = 8, 16, 2
FAR = (4, 3, 5, 2, 6, 1, 7)
ORDER = tuple((xx, i) for i, xx in enumerate((0, 1, 7, 2, 6, 3, 5, 4)))


def iota(shape, dim):
    return lax.broadcasted_iota(jnp.int32, shape, dim)


def beam_matrix(w_ref):
    elems = w_ref.shape[1] // NB
    spread = (iota((CH, elems * CH), 1) % CH == iota((CH, elems * CH), 0)).astype(F32).astype(BF16)
    shape = (NB * elems, elems * CH)
    own = iota(shape, 0) % elems == iota(shape, 1) // CH
    shape = (2 * NB, NB * elems)
    pick = (iota(shape, 0) % NB == iota(shape, 1) // elems).astype(F32).astype(BF16)
    flat = []
    for part in range(2):
        wide = jnp.dot(w_ref[part], spread, preferred_element_type=F32)
        wide = jnp.where(own, wide, 0.0).astype(BF16)
        flat.append(jnp.dot(pick, wide, preferred_element_type=F32))
    top = iota(flat[0].shape, 0) < NB
    left = jnp.where(top, flat[0], -flat[1])
    right = jnp.where(top, flat[1], flat[0])
    both = jnp.concatenate([left, right], axis=1)
    lane = iota(both.shape, 1) % CH
    return jnp.concatenate(
        [jnp.where(lane == c, both, 0.0).astype(BF16) for c in range(CH)], axis=0
    )


def kernel(scale, volt_hbm, w_hbm, ret, early, volt, w, part32, part16, got, mine, cols, rows, res,
           in_sem, es_sem, er_sem, gs_sem, cr_sem, rr_sem, ts_sem, tr_sem, here, zs_sem, near, xs_sem):
    s, e = lax.axis_index("stn"), lax.axis_index("elem")
    k, x = lax.rem(s, 2), lax.rem(s // 2, RING)
    z, y = lax.rem(s // (2 * RING), RING), s // (2 * RING * RING)
    r_own, w_own = x + k * (z - x), z + k * (x - z)

    def at(yy, rr, ww, kk):
        zz, xx = ww + k * (rr - ww), rr + k * (ww - rr)
        return {"stn": ((yy * RING + zz) * RING + xx) * 2 + kk, "elem": e}

    def along_r(dy, d, kk):
        return at(lax.rem(y + dy, YS), lax.rem(r_own + d, RING), w_own, kk)

    def along_w(dy, d, kk):
        return at(lax.rem(y + dy, YS), r_own, lax.rem(w_own + d, RING), kk)

    partner = at(y, r_own, w_own, 1 - k)
    facing = at(1 - y, r_own, w_own, k)

    load_v = pltpu.make_async_copy(volt_hbm, volt, in_sem.at[0])
    load_w = pltpu.make_async_copy(w_hbm, w, in_sem.at[1])
    load_w.start()
    load_v.start()

    def device(zz, xx, kk):
        return {"stn": ((y * RING + zz) * RING + xx) * 2 + kk, "elem": e}

    my_place = jnp.where(x <= RING // 2, jnp.maximum(2 * x - 1, 0), 2 * (RING - x))
    barrier = pltpu.get_barrier_semaphore()
    peers = 0

    def greet(peer):
        nonlocal peers
        pl.semaphore_signal(barrier, inc=1, device_id=peer, device_id_type=MESH)
        peers += 1

    for d in (2, 1, 3):
        greet({"stn": s, "elem": lax.rem(e + d, PARTS)})
    for xx, place_of in ORDER:
        @pl.when(place_of > my_place)
        def _():
            for kk in range(CORES):
                pl.semaphore_signal(barrier, inc=1, device_id=device(z, xx, kk), device_id_type=MESH)
    greet(facing)
    greet(partner)
    for zz in range(1, RING):
        @pl.when(zz > z)
        def _():
            for kk in range(CORES):
                pl.semaphore_signal(barrier, inc=1, device_id=device(zz, x, kk), device_id_type=MESH)

    load_w.wait()
    matrix = beam_matrix(w)
    load_v.wait()
    partial = jnp.dot(matrix, volt[...], preferred_element_type=F32)
    part32[...] = partial
    part16[...] = partial.astype(part16.dtype)
    pl.semaphore_wait(barrier, peers + CORES * (z + my_place))
    for xx, place_of in ORDER:
        @pl.when(place_of < my_place)
        def _():
            for kk in range(CORES):
                pl.semaphore_signal(near.at[x], inc=1, device_id=device(z, xx, kk), device_id_type=MESH)
    for zz in range(RING - 1):
        @pl.when(zz < z)
        def _():
            for kk in range(CORES):
                pl.semaphore_signal(here.at[z], inc=1, device_id=device(zz, x, kk), device_id_type=MESH)

    quarter = part32.shape[0] // PARTS
    piece = quarter // 2

    def rows_of(q, h):
        return pl.ds(pl.multiple_of(q * quarter + h * piece, piece), piece)

    sends, partials = [], ([], [])
    for turn, h in enumerate((0, 1)):
        for d in (2, 1, 3):
            q = lax.rem(e + d, PARTS)
            copy = pltpu.make_async_remote_copy(
                src_ref=part16.at[rows_of(q, h)],
                dst_ref=got.at[d - 1, turn],
                send_sem=es_sem.at[d - 1, turn],
                recv_sem=er_sem.at[d - 1, turn],
                device_id={"stn": s, "elem": q},
                device_id_type=MESH,
            )
            copy.start()
            sends.append(copy)
            partials[turn].append(copy)

    def add_up(turn, h):
        total = part32[rows_of(e, h)]
        for copy in partials[turn][::-1]:
            copy.wait_recv()
        for d in (1, 2, 3):
            total = total + got[d - 1, turn].astype(F32)
        mine[h] = total.astype(BF16).reshape(mine.shape[1:])

    count = 0

    def send(src, dst, sem, device):
        nonlocal count
        copy = pltpu.make_async_remote_copy(
            src_ref=src, dst_ref=dst, send_sem=gs_sem.at[count], recv_sem=sem,
            device_id=device, device_id_type=MESH,
        )
        copy.start()
        sends.append(copy)
        count += 1

    col, row = r_own * 2 + k, w_own * 2 + k
    other_col, other_row = w_own * 2 + k, r_own * 2 + k
    add_up(0, 0)

    def in_plane(xx, h):
        slot = x * 2 + k
        dst, sem = (rows.at[slot], rr_sem.at[slot]) if h else (cols.at[y, slot], cr_sem.at[y, slot])
        return pltpu.make_async_remote_copy(
            src_ref=mine.at[h], dst_ref=dst, send_sem=xs_sem.at[xx, h], recv_sem=sem,
            device_id=device(z, xx, h), device_id_type=MESH,
        )

    for xx, place_of in ORDER:
        @pl.when(place_of > my_place)
        def _():
            pl.semaphore_wait(near.at[xx], CORES)

        @pl.when(xx != x)
        def _():
            in_plane(xx, 0).start()
    add_up(1, 1)
    for xx in range(RING):
        @pl.when(xx != x)
        def _():
            in_plane(xx, 1).start()
    other = mine.at[1 - k]
    send(other, cols.at[y, other_col], cr_sem.at[y, other_col], partner)
    send(other, rows.at[other_row], rr_sem.at[other_row], partner)

    def to_plane(zz):
        slot = z * 2 + k
        return [
            pltpu.make_async_remote_copy(
                src_ref=mine.at[1 - h], dst_ref=dst, send_sem=zs_sem.at[zz, h], recv_sem=sem,
                device_id=device(zz, x, 1 - h), device_id_type=MESH,
            )
            for h, (dst, sem) in enumerate(((cols.at[y, slot], cr_sem.at[y, slot]), (rows.at[slot], rr_sem.at[slot])))
        ]

    for zz in range(RING):
        @pl.when(zz > z)
        def _():
            pl.semaphore_wait(here.at[zz], CORES)

        @pl.when(zz != z)
        def _():
            for copy in to_plane(zz):
                copy.start()
    half = mine[k]
    cols[y, col] = half
    rows[row] = half

    def landed(dst, sem):
        pltpu.make_async_remote_copy(
            src_ref=dst, dst_ref=dst, send_sem=gs_sem.at[0], recv_sem=sem,
            device_id=partner, device_id_type=MESH,
        ).wait_recv()

    def rows_landed():
        landed(rows.at[w_own * 2 + 1 - k], rr_sem.at[w_own * 2 + 1 - k])
        for d in FAR[::-1]:
            for kk in range(2):
                slot = lax.rem(w_own + d, RING) * 2 + kk
                landed(rows.at[slot], rr_sem.at[slot])

    cross = (((1,), (1,)), ((), ()))
    back = 0
    turned = [None] * HALF
    for i, d in enumerate((0,) + FAR[::-1]):
        rr = lax.rem(x + d, RING)
        rr = rr + k * (i - rr)
        base = rr * 2

        @pl.when(rr != r_own)
        def _():
            for slot in (base, base + 1):
                landed(cols.at[y, slot], cr_sem.at[y, slot])

        @pl.when(rr == r_own)
        def _():
            landed(cols.at[y, base + 1 - k], cr_sem.at[y, base + 1 - k])

        pair = cols.at[y, pl.ds(base, 2)]
        send(pair, pair, cr_sem.at[y, base], facing)
    rows_landed()
    for dy in range(YS):
        yy = lax.rem(y + dy, YS)
        if dy == 1:
            for base in range(0, 2 * RING, 2):
                landed(cols.at[yy, pl.ds(base, 2)], cr_sem.at[yy, base])
        for c in range(HALF):
            tile = rows[:, c]
            n, _, samples = tile.shape
            if dy == 0:
                wide = tile.astype(F32).reshape(n, 2, NB, samples)
                wide = jnp.concatenate([wide[:, 1:], -wide[:, :1]], axis=1)
                turned[c] = wide.reshape(n * 2 * NB, samples).astype(BF16)
            wide = cols[yy, :, c].astype(F32).reshape(RING * CORES, 2, NB, samples)
            real, imag = (wide[:, p].reshape(RING * CORES * NB, samples).astype(BF16) for p in range(2))
            prod = lax.dot_general(tile.reshape(n * 2 * NB, samples), real, cross, preferred_element_type=F32)
            prod += lax.dot_general(turned[c], imag, cross, preferred_element_type=F32)
            res[yy, :, c] = (prod * scale).astype(BF16).reshape(n, 2 * NB, -1)
        for d in tuple(range(1, RING)) + (0,):
            slot = lax.rem(w_own + d, RING) * 2
            for kk in (1 - k,) if d == 0 else (0, 1):
                copy = pltpu.make_async_remote_copy(
                    src_ref=res.at[yy, slot + kk], dst_ref=ret.at[k, yy, w_own], send_sem=ts_sem.at[back],
                    recv_sem=tr_sem.at[k, yy, w_own], device_id=along_w(0, d, kk), device_id_type=MESH,
                )
                copy.start()
                sends.append(copy)
                back += 1
        ret[k, yy, w_own] = res[yy, row]

    for copy in sends:
        copy.wait_send()
    for i in range(RING):
        @pl.when(i != z)
        def _():
            for copy in to_plane(i):
                copy.wait_send()

        @pl.when(i != x)
        def _():
            for h in range(2):
                in_plane(i, h).wait_send()

    for dy in range(YS):
        yy = lax.rem(y + dy, YS)
        for d in (0,) + FAR[::-1]:
            if d:
                slot = lax.rem(w_own + d, RING)
                landed(ret.at[k, yy, slot], tr_sem.at[k, yy, slot])
            slot = lax.rem(r_own + d, RING)
            landed(ret.at[1 - k, yy, slot], tr_sem.at[1 - k, yy, slot])
        if dy == 0:
            unpack(ret, early, yy)


def unpack(ret, out, yy):
    lanes = ret.shape[-1]
    group = iota((2 * NB, lanes), 1) // (CORES * NB)
    for h in range(2):
        for c in range(HALF):
            tiles = [ret[h, yy, i, c].astype(F32) for i in range(RING)]
            for bit in (1, 2, 4) if h else ():
                high = (group // bit) % 2 == 1
                swapped = list(tiles)
                for i in range(RING):
                    if i & bit:
                        continue
                    a, b = tiles[i], tiles[i | bit]
                    shift = bit * CORES * NB
                    swapped[i] = jnp.where(high, pltpu.roll(b, shift, 1), a)
                    swapped[i | bit] = jnp.where(high, b, pltpu.roll(a, lanes - shift, 1))
                tiles = swapped
            for i in range(RING):
                for part in range(2):
                    out[part, h * HALF + c, :, pl.ds(i * lanes, lanes)] = tiles[i][part * NB:(part + 1) * NB]


def place(out_hbm, yy):
    width = out_hbm.shape[3] // YS
    return out_hbm.at[:, :, :, pl.ds(pl.multiple_of(yy * width, width), width)]


def finish(ret, early, out_hbm, out, sem):
    y = lax.axis_index("stn") // (2 * RING * RING)
    first = pltpu.make_async_copy(early, place(out_hbm, y), sem.at[0])
    first.start()
    unpack(ret, out, 1 - y)
    last = pltpu.make_async_copy(out, place(out_hbm, 1 - y), sem.at[1])
    last.start()
    first.wait()
    last.wait()


def body(voltages, weights):
    samples = voltages.shape[4]
    elems = voltages.shape[2]
    mine_ch = CH // PARTS
    volt = voltages.reshape(2 * elems * CH, samples)
    w = weights.reshape(2, NB * elems, CH)
    lanes = RING * CORES * NB
    block = (HALF, 2 * NB, samples)
    result = (HALF, 2 * NB, lanes)
    gathers = RING + 2
    dma = pltpu.SemaphoreType.DMA
    shape = (2, mine_ch, NB, YS * RING * lanes)
    half = shape[:3] + (RING * lanes,)
    ret, early = pl.pallas_call(
        functools.partial(kernel, 1.0 / samples),
        out_shape=(pltpu.VMEM((2, YS, RING) + result, BF16), pltpu.VMEM(half, F32)),
        in_specs=[pl.BlockSpec(memory_space=pl.ANY)] * 2,
        out_specs=(pl.BlockSpec(memory_space=pltpu.VMEM),) * 2,
        scratch_shapes=[
            pltpu.VMEM(volt.shape, BF16),
            pltpu.VMEM(w.shape, BF16),
            pltpu.VMEM((CH * 2 * NB, samples), F32),
            pltpu.VMEM((CH * 2 * NB, samples), BF16),
            pltpu.VMEM((PARTS - 1, 2, HALF * 2 * NB, samples), BF16),
            pltpu.VMEM((2,) + block, BF16),
            pltpu.VMEM((YS, RING * CORES) + block, BF16),
            pltpu.VMEM((RING * CORES,) + block, BF16),
            pltpu.VMEM((YS, RING * CORES) + result, BF16),
            dma((2,)),
            dma((PARTS - 1, 2)),
            dma((PARTS - 1, 2)),
            dma((gathers,)),
            dma((YS, RING * CORES)),
            dma((RING * CORES,)),
            dma((YS * RING * CORES,)),
            dma((2, YS, RING)),
            pltpu.SemaphoreType.REGULAR((RING,)),
            dma((RING, 2)),
            pltpu.SemaphoreType.REGULAR((RING,)),
            dma((RING, 2)),
        ],
        compiler_params=pltpu.CompilerParams(collective_id=0, has_side_effects=True),
    )(volt, w)
    return pl.pallas_call(
        finish,
        out_shape=jax.ShapeDtypeStruct(shape, F32),
        in_specs=[pl.BlockSpec(memory_space=pltpu.VMEM)] * 2,
        out_specs=pl.BlockSpec(memory_space=pl.ANY),
        scratch_shapes=[pltpu.VMEM(half, F32), dma((2,))],
    )(*(pltpu.with_memory_space_constraint(a, pltpu.VMEM) for a in (ret, early)))


def solution(mesh):
    placed = (P(None, "stn", "elem", None, None), P(None, None, "elem", None))
    return jax.shard_map(
        body, mesh=mesh, in_specs=placed, out_specs=P(None, "elem", "stn", None), check_vma=False
    )
```

```python
import functools

import jax
import jax.numpy as jnp
from jax import lax
from jax.experimental import pallas as pl
from jax.experimental.pallas import tpu as pltpu
from jax.sharding import PartitionSpec as P

MESH = pl.DeviceIdType.MESH
F32, BF16 = jnp.float32, jnp.bfloat16
RING, YS, CORES, PARTS = 8, 2, 2, 4
NB, CH, HALF = 8, 16, 2
FAR = (4, 3, 5, 2, 6, 1, 7)
ORDER = tuple((xx, i) for i, xx in enumerate((0, 1, 7, 2, 6, 3, 5, 4)))


def iota(shape, dim):
    return lax.broadcasted_iota(jnp.int32, shape, dim)


def beam_matrix(w_ref):
    elems = w_ref.shape[1] // NB
    spread = (iota((CH, elems * CH), 1) % CH == iota((CH, elems * CH), 0)).astype(F32).astype(BF16)
    shape = (NB * elems, elems * CH)
    own = iota(shape, 0) % elems == iota(shape, 1) // CH
    shape = (2 * NB, NB * elems)
    pick = (iota(shape, 0) % NB == iota(shape, 1) // elems).astype(F32).astype(BF16)
    flat = []
    for part in range(2):
        wide = jnp.dot(w_ref[part], spread, preferred_element_type=F32)
        wide = jnp.where(own, wide, 0.0).astype(BF16)
        flat.append(jnp.dot(pick, wide, preferred_element_type=F32))
    top = iota(flat[0].shape, 0) < NB
    left = jnp.where(top, flat[0], -flat[1])
    right = jnp.where(top, flat[1], flat[0])
    both = jnp.concatenate([left, right], axis=1)
    lane = iota(both.shape, 1) % CH
    return jnp.concatenate(
        [jnp.where(lane == c, both, 0.0).astype(BF16) for c in range(CH)], axis=0
    )


def kernel(scale, volt_hbm, w_hbm, ret, early, volt, w, part32, part16, got, mine, cols, rows, res,
           in_sem, es_sem, er_sem, gs_sem, cr_sem, rr_sem, ts_sem, tr_sem, here, zs_sem, near, xs_sem):
    s, e = lax.axis_index("stn"), lax.axis_index("elem")
    k, x = lax.rem(s, 2), lax.rem(s // 2, RING)
    z, y = lax.rem(s // (2 * RING), RING), s // (2 * RING * RING)
    r_own, w_own = x + k * (z - x), z + k * (x - z)

    def at(yy, rr, ww, kk):
        zz, xx = ww + k * (rr - ww), rr + k * (ww - rr)
        return {"stn": ((yy * RING + zz) * RING + xx) * 2 + kk, "elem": e}

    def along_r(dy, d, kk):
        return at(lax.rem(y + dy, YS), lax.rem(r_own + d, RING), w_own, kk)

    def along_w(dy, d, kk):
        return at(lax.rem(y + dy, YS), r_own, lax.rem(w_own + d, RING), kk)

    partner = at(y, r_own, w_own, 1 - k)
    facing = at(1 - y, r_own, w_own, k)

    load_v = pltpu.make_async_copy(volt_hbm, volt, in_sem.at[0])
    load_w = pltpu.make_async_copy(w_hbm, w, in_sem.at[1])
    load_w.start()
    load_v.start()

    def device(zz, xx, kk):
        return {"stn": ((y * RING + zz) * RING + xx) * 2 + kk, "elem": e}

    my_place = jnp.where(x <= RING // 2, jnp.maximum(2 * x - 1, 0), 2 * (RING - x))
    barrier = pltpu.get_barrier_semaphore()
    peers = 0

    def greet(peer):
        nonlocal peers
        pl.semaphore_signal(barrier, inc=1, device_id=peer, device_id_type=MESH)
        peers += 1

    for d in (2, 1, 3):
        greet({"stn": s, "elem": lax.rem(e + d, PARTS)})
    for xx, place_of in ORDER:
        @pl.when(place_of > my_place)
        def _():
            for kk in range(CORES):
                pl.semaphore_signal(barrier, inc=1, device_id=device(z, xx, kk), device_id_type=MESH)
    greet(facing)
    greet(partner)
    for zz in range(1, RING):
        @pl.when(zz > z)
        def _():
            for kk in range(CORES):
                pl.semaphore_signal(barrier, inc=1, device_id=device(zz, x, kk), device_id_type=MESH)

    load_w.wait()
    matrix = beam_matrix(w)
    load_v.wait()
    partial = jnp.dot(matrix, volt[...], preferred_element_type=F32)
    part32[...] = partial
    part16[...] = partial.astype(part16.dtype)
    pl.semaphore_wait(barrier, peers + CORES * (z + my_place))
    for xx, place_of in ORDER:
        @pl.when(place_of < my_place)
        def _():
            for kk in range(CORES):
                pl.semaphore_signal(near.at[x], inc=1, device_id=device(z, xx, kk), device_id_type=MESH)
    for zz in range(RING - 1):
        @pl.when(zz < z)
        def _():
            for kk in range(CORES):
                pl.semaphore_signal(here.at[z], inc=1, device_id=device(zz, x, kk), device_id_type=MESH)

    quarter = part32.shape[0] // PARTS
    piece = quarter // 2

    def rows_of(q, h):
        return pl.ds(pl.multiple_of(q * quarter + h * piece, piece), piece)

    sends, partials = [], ([], [])
    for turn, h in enumerate((0, 1)):
        for d in (2, 1, 3):
            q = lax.rem(e + d, PARTS)
            copy = pltpu.make_async_remote_copy(
                src_ref=part16.at[rows_of(q, h)],
                dst_ref=got.at[d - 1, turn],
                send_sem=es_sem.at[d - 1, turn],
                recv_sem=er_sem.at[d - 1, turn],
                device_id={"stn": s, "elem": q},
                device_id_type=MESH,
            )
            copy.start()
            sends.append(copy)
            partials[turn].append(copy)

    def add_up(turn, h):
        total = part32[rows_of(e, h)]
        for copy in partials[turn][::-1]:
            copy.wait_recv()
        for d in (1, 2, 3):
            total = total + got[d - 1, turn].astype(F32)
        mine[h] = total.astype(BF16).reshape(mine.shape[1:])

    count = 0

    def send(src, dst, sem, device):
        nonlocal count
        copy = pltpu.make_async_remote_copy(
            src_ref=src, dst_ref=dst, send_sem=gs_sem.at[count], recv_sem=sem,
            device_id=device, device_id_type=MESH,
        )
        copy.start()
        sends.append(copy)
        count += 1

    col, row = r_own * 2 + k, w_own * 2 + k
    other_col, other_row = w_own * 2 + k, r_own * 2 + k
    add_up(0, 0)

    def in_plane(xx, h):
        slot = x * 2 + k
        dst, sem = (rows.at[slot], rr_sem.at[slot]) if h else (cols.at[y, slot], cr_sem.at[y, slot])
        return pltpu.make_async_remote_copy(
            src_ref=mine.at[h], dst_ref=dst, send_sem=xs_sem.at[xx, h], recv_sem=sem,
            device_id=device(z, xx, h), device_id_type=MESH,
        )

    for xx, place_of in ORDER:
        @pl.when(place_of > my_place)
        def _():
            pl.semaphore_wait(near.at[xx], CORES)

        @pl.when(xx != x)
        def _():
            in_plane(xx, 0).start()
    add_up(1, 1)
    for xx in range(RING):
        @pl.when(xx != x)
        def _():
            in_plane(xx, 1).start()
    other = mine.at[1 - k]
    send(other, cols.at[y, other_col], cr_sem.at[y, other_col], partner)
    send(other, rows.at[other_row], rr_sem.at[other_row], partner)

    def to_plane(zz):
        slot = z * 2 + k
        return [
            pltpu.make_async_remote_copy(
                src_ref=mine.at[1 - h], dst_ref=dst, send_sem=zs_sem.at[zz, h], recv_sem=sem,
                device_id=device(zz, x, 1 - h), device_id_type=MESH,
            )
            for h, (dst, sem) in enumerate(((cols.at[y, slot], cr_sem.at[y, slot]), (rows.at[slot], rr_sem.at[slot])))
        ]

    for zz in range(RING):
        @pl.when(zz > z)
        def _():
            pl.semaphore_wait(here.at[zz], CORES)

        @pl.when(zz != z)
        def _():
            for copy in to_plane(zz):
                copy.start()
    half = mine[k]
    cols[y, col] = half
    rows[row] = half

    def landed(dst, sem):
        pltpu.make_async_remote_copy(
            src_ref=dst, dst_ref=dst, send_sem=gs_sem.at[0], recv_sem=sem,
            device_id=partner, device_id_type=MESH,
        ).wait_recv()

    cross = (((1,), (1,)), ((), ()))
    for i, d in enumerate((0,) + FAR[::-1]):
        rr = lax.rem(x + d, RING)
        rr = rr + k * (i - rr)
        base = rr * 2

        @pl.when(rr != r_own)
        def _():
            for slot in (base, base + 1):
                landed(cols.at[y, slot], cr_sem.at[y, slot])

        @pl.when(rr == r_own)
        def _():
            landed(cols.at[y, base + 1 - k], cr_sem.at[y, base + 1 - k])

        pair = cols.at[y, pl.ds(base, 2)]
        send(pair, pair, cr_sem.at[y, base], facing)
    def back(dy, pos, kk):
        yy = lax.rem(y + dy, YS)
        return pltpu.make_async_remote_copy(
            src_ref=res.at[yy, pos * 2 + kk], dst_ref=ret.at[k, yy, w_own],
            send_sem=ts_sem.at[(dy * RING + pos) * 2 + kk], recv_sem=tr_sem.at[k, yy, w_own],
            device_id=at(y, r_own, pos, kk), device_id_type=MESH,
        )

    for low in (True, False):
        positions = range(RING // 2) if low else range(RING // 2, RING)
        first = positions[0] * 2
        for pos in positions:
            @pl.when(pos != w_own)
            def _():
                for slot in (pos * 2, pos * 2 + 1):
                    landed(rows.at[slot], rr_sem.at[slot])

            @pl.when(pos == w_own)
            def _():
                landed(rows.at[pos * 2 + 1 - k], rr_sem.at[pos * 2 + 1 - k])
        for dy in range(YS):
            yy = lax.rem(y + dy, YS)
            if low and dy == 1:
                for base in range(0, 2 * RING, 2):
                    landed(cols.at[yy, pl.ds(base, 2)], cr_sem.at[yy, base])
            part = slice(first, first + RING)
            for c in range(HALF):
                tile = rows[part, c]
                n, _, samples = tile.shape
                wide = tile.astype(F32).reshape(n, 2, NB, samples)
                wide = jnp.concatenate([wide[:, 1:], -wide[:, :1]], axis=1)
                turned = wide.reshape(n * 2 * NB, samples).astype(BF16)
                wide = cols[yy, :, c].astype(F32).reshape(RING * CORES, 2, NB, samples)
                real, imag = (wide[:, p].reshape(RING * CORES * NB, samples).astype(BF16) for p in range(2))
                prod = lax.dot_general(tile.reshape(n * 2 * NB, samples), real, cross, preferred_element_type=F32)
                prod += lax.dot_general(turned, imag, cross, preferred_element_type=F32)
                res[yy, part, c] = (prod * scale).astype(BF16).reshape(n, 2 * NB, -1)
            for pos in positions:
                @pl.when(pos != w_own)
                def _():
                    for kk in range(CORES):
                        back(dy, pos, kk).start()

                @pl.when(pos == w_own)
                def _():
                    back(dy, pos, 1 - k).start()
                    ret[k, yy, w_own] = res[yy, row]

    for copy in sends:
        copy.wait_send()
    for i in range(RING):
        @pl.when(i != z)
        def _():
            for copy in to_plane(i):
                copy.wait_send()

        @pl.when(i != x)
        def _():
            for h in range(2):
                in_plane(i, h).wait_send()

        @pl.when(i != w_own)
        def _():
            for dy in range(YS):
                for kk in range(CORES):
                    back(dy, i, kk).wait_send()

        @pl.when(i == w_own)
        def _():
            for dy in range(YS):
                back(dy, i, 1 - k).wait_send()

    for dy in range(YS):
        yy = lax.rem(y + dy, YS)
        for d in (0,) + FAR[::-1]:
            if d:
                slot = lax.rem(w_own + d, RING)
                landed(ret.at[k, yy, slot], tr_sem.at[k, yy, slot])
            slot = lax.rem(r_own + d, RING)
            landed(ret.at[1 - k, yy, slot], tr_sem.at[1 - k, yy, slot])
        if dy == 0:
            unpack(ret, early, yy)


def unpack(ret, out, yy):
    lanes = ret.shape[-1]
    group = iota((2 * NB, lanes), 1) // (CORES * NB)
    for h in range(2):
        for c in range(HALF):
            tiles = [ret[h, yy, i, c].astype(F32) for i in range(RING)]
            for bit in (1, 2, 4) if h else ():
                high = (group // bit) % 2 == 1
                swapped = list(tiles)
                for i in range(RING):
                    if i & bit:
                        continue
                    a, b = tiles[i], tiles[i | bit]
                    shift = bit * CORES * NB
                    swapped[i] = jnp.where(high, pltpu.roll(b, shift, 1), a)
                    swapped[i | bit] = jnp.where(high, b, pltpu.roll(a, lanes - shift, 1))
                tiles = swapped
            for i in range(RING):
                for part in range(2):
                    out[part, h * HALF + c, :, pl.ds(i * lanes, lanes)] = tiles[i][part * NB:(part + 1) * NB]


def place(out_hbm, yy):
    width = out_hbm.shape[3] // YS
    return out_hbm.at[:, :, :, pl.ds(pl.multiple_of(yy * width, width), width)]


def finish(ret, early, out_hbm, out, sem):
    y = lax.axis_index("stn") // (2 * RING * RING)
    first = pltpu.make_async_copy(early, place(out_hbm, y), sem.at[0])
    first.start()
    unpack(ret, out, 1 - y)
    last = pltpu.make_async_copy(out, place(out_hbm, 1 - y), sem.at[1])
    last.start()
    first.wait()
    last.wait()


def body(voltages, weights):
    samples = voltages.shape[4]
    elems = voltages.shape[2]
    mine_ch = CH // PARTS
    volt = voltages.reshape(2 * elems * CH, samples)
    w = weights.reshape(2, NB * elems, CH)
    lanes = RING * CORES * NB
    block = (HALF, 2 * NB, samples)
    result = (HALF, 2 * NB, lanes)
    gathers = RING + 2
    dma = pltpu.SemaphoreType.DMA
    shape = (2, mine_ch, NB, YS * RING * lanes)
    half = shape[:3] + (RING * lanes,)
    ret, early = pl.pallas_call(
        functools.partial(kernel, 1.0 / samples),
        out_shape=(pltpu.VMEM((2, YS, RING) + result, BF16), pltpu.VMEM(half, F32)),
        in_specs=[pl.BlockSpec(memory_space=pl.ANY)] * 2,
        out_specs=(pl.BlockSpec(memory_space=pltpu.VMEM),) * 2,
        scratch_shapes=[
            pltpu.VMEM(volt.shape, BF16),
            pltpu.VMEM(w.shape, BF16),
            pltpu.VMEM((CH * 2 * NB, samples), F32),
            pltpu.VMEM((CH * 2 * NB, samples), BF16),
            pltpu.VMEM((PARTS - 1, 2, HALF * 2 * NB, samples), BF16),
            pltpu.VMEM((2,) + block, BF16),
            pltpu.VMEM((YS, RING * CORES) + block, BF16),
            pltpu.VMEM((RING * CORES,) + block, BF16),
            pltpu.VMEM((YS, RING * CORES) + result, BF16),
            dma((2,)),
            dma((PARTS - 1, 2)),
            dma((PARTS - 1, 2)),
            dma((gathers,)),
            dma((YS, RING * CORES)),
            dma((RING * CORES,)),
            dma((YS * RING * CORES,)),
            dma((2, YS, RING)),
            pltpu.SemaphoreType.REGULAR((RING,)),
            dma((RING, 2)),
            pltpu.SemaphoreType.REGULAR((RING,)),
            dma((RING, 2)),
        ],
        compiler_params=pltpu.CompilerParams(collective_id=0, has_side_effects=True),
    )(volt, w)
    return pl.pallas_call(
        finish,
        out_shape=jax.ShapeDtypeStruct(shape, F32),
        in_specs=[pl.BlockSpec(memory_space=pltpu.VMEM)] * 2,
        out_specs=pl.BlockSpec(memory_space=pl.ANY),
        scratch_shapes=[pltpu.VMEM(half, F32), dma((2,))],
    )(*(pltpu.with_memory_space_constraint(a, pltpu.VMEM) for a in (ret, early)))


def solution(mesh):
    placed = (P(None, "stn", "elem", None, None), P(None, None, "elem", None))
    return jax.shard_map(
        body, mesh=mesh, in_specs=placed, out_specs=P(None, "elem", "stn", None), check_vma=False
    )
```
